32 devices in a mesh: sp: 16 (over z, y, core), flt: 2 (over x).
Axes of the slice: x: 2, y: 2, z: 4, core: 2. Of those that a mesh axis runs over, the one named last changes fastest.
Arguments:
- activations: bfloat16 [32, 16, 8, 256], P('sp', 'flt'), may hold values from -6 to 6
- w_first: bfloat16 [256, 3, 3, 3, 256], P('flt'), may hold values from -0.078125 to 0.078125
- w_second: bfloat16 [256, 3, 3, 3, 256], P('flt'), may hold values from -0.078125 to 0.078125
- cotangent: bfloat16 [16, 8, 4, 256], P('sp', 'flt'), may hold values from -6 to 6
Outputs:
- section_out: float32 [16, 8, 4, 256], P('sp', 'flt')
- grad_input: float32 [32, 16, 8, 256], P('sp', 'flt')
- grad_first: float32 [256, 3, 3, 3, 256], P('flt')
- grad_second: float32 [256, 3, 3, 3, 256], P('flt')
The draws below stay inside these ranges and needn't reach their ends.
All inputs are finite; a program needn't handle non-finite values.
Results may differ from the reference program's by a relative error of at most 0.0045.
Values may be sent and summed in bfloat16 or wider, within the bound.
A program may use at most 64 MiB of HBM per device.

```python
import jax
import jax.numpy as jnp
from jax import lax

C = 256
Z = 8
X = 32
Y = 16


def block_scale(own_key, shape, shards, least, largest):
    def one(axis_at, shards_of):
        draws = jax.random.uniform(jax.random.fold_in(jax.random.fold_in(own_key, 6), axis_at), (shards_of,), jnp.float32, least / len(shards), largest / len(shards))
        return jnp.repeat(jnp.exp(draws), shape[axis_at] // shards_of).reshape((-1,) + (1,) * (len(shape) - axis_at - 1))

    level = one(*shards[0])
    for cut in shards[1:]:
        level = level * one(*cut)
    return level


def gaussian(key, dims, spread, bound, pieces=(), held_as=jnp.bfloat16):
    entries = spread * jax.random.normal(key, dims, jnp.float32)
    if pieces:
        entries = entries * block_scale(key, dims, pieces, -0.22, 0.18)
    return jnp.clip(entries, -bound, bound).astype(held_as)


def setup_inputs(seed: int = 0) -> dict:
    seeds = jax.random.split(jax.random.key(seed), 5)
    return {
        "activations": gaussian(seeds[0], (X, Y, Z, C), 1.0, 6.0, ((0, 16), (1, 2))),
        "w_first": gaussian(seeds[1], (C, 3, 3, 3, C), (27 * C) ** -0.5, 0.078125, ((0, 2),)),
        "w_second": gaussian(seeds[2], (C, 3, 3, 3, C), (27 * C) ** -0.5, 0.078125, ((0, 2),)),
        "cotangent": gaussian(seeds[3], (X // 2, Y // 2, Z // 2, C), 1.0, 6.0, ((0, 16), (1, 2))),
    }


def as_taps(kernel):
    return jnp.transpose(kernel, (1, 2, 3, 4, 0))

def conv_same(field, kernel):
    return lax.conv_general_dilated(field[None].astype(jnp.float32), as_taps(kernel).astype(jnp.float32), (1, 1, 1), ((1, 1), (1, 1), (1, 1)), dimension_numbers=('NDHWC', 'DHWIO', 'NDHWC'), precision=lax.Precision.HIGHEST)[0]

def conv_down(field, kernel):
    return lax.conv_general_dilated(field[None].astype(jnp.float32), as_taps(kernel).astype(jnp.float32), (2, 2, 2), ((1, 0), (1, 0), (1, 0)), dimension_numbers=('NDHWC', 'DHWIO', 'NDHWC'), precision=lax.Precision.HIGHEST)[0]

def silu_slope(value):
    sig = jax.nn.sigmoid(value)
    return sig * (1.0 + value * (1.0 - sig))

def reference(activations, w_first, w_second, cotangent):
    first_pre = conv_same(activations, w_first)
    hidden = jax.nn.silu(first_pre).astype(jnp.bfloat16)
    second_pre = conv_down(hidden, w_second)
    section_out = jax.nn.silu(second_pre)
    second_err = (cotangent.astype(jnp.float32) * silu_slope(second_pre)).astype(jnp.bfloat16)
    unused_two, back_two = jax.vjp(conv_down, hidden.astype(jnp.float32), w_second.astype(jnp.float32))
    hidden_err, grad_second = back_two(second_err.astype(jnp.float32))
    first_err = (hidden_err * silu_slope(first_pre)).astype(jnp.bfloat16)
    unused_one, back_one = jax.vjp(conv_same, activations.astype(jnp.float32), w_first.astype(jnp.float32))
    grad_input, grad_first = back_one(first_err.astype(jnp.float32))
    return (section_out, grad_input, grad_first, grad_second)
```

```python
import functools

import jax
import jax.numpy as jnp
from jax import lax
from jax.experimental import pallas as pl
from jax.experimental.pallas import tpu as pltpu
from jax.sharding import PartitionSpec as P

MESH = pl.DeviceIdType.MESH
VMEM = pl.BlockSpec(memory_space=pltpu.VMEM)
ROOM = 62 * 1024 * 1024


def remote(src, dst, send, recv, place):
    return pltpu.make_async_remote_copy(
        src_ref=src, dst_ref=dst, send_sem=send, recv_sem=recv, device_id=place, device_id_type=MESH
    )


def greet(places):
    barrier = pltpu.get_barrier_semaphore()
    for place in places:
        pl.semaphore_signal(barrier, inc=1, device_id=place, device_id_type=MESH)
    pl.semaphore_wait(barrier, len(places))


def line_kernel(count, own, out, local, recv, send_z, send_y, send_c):
    here, other = lax.axis_index("sp"), lax.axis_index("flt")
    deep = count // 4
    z, y, core = here // 4, (here // 2) % 2, here % 2

    def spot(zz, yy, cc):
        return (zz * 2 + yy) * 2 + cc

    far = [lax.rem(z + step, deep) for step in range(1, deep)]
    to_y = (spot(z, 1 - y, core), other)
    to_c = (spot(z, y, 1 - core), other)
    greet([(spot(zz, y, core), other) for zz in far] + [to_y, to_c])
    sends = []

    def push(src, slot, send, place):
        copy = remote(src, out.at[slot], send, recv.at[slot], place)
        copy.start()
        sends.append(copy)

    def arrived(slot):
        remote(own, out.at[slot], send_y.at[0], recv.at[slot], to_y).wait_recv()

    for n, zz in enumerate(far):
        push(own, here, send_z.at[n], (spot(zz, y, core), other))
    push(own, here, send_y.at[0], to_y)
    push(own, here, send_c.at[0], to_c)
    keep = pltpu.make_async_copy(own, out.at[here], local)
    keep.start()
    for n in range(1, deep):
        slot = spot(lax.rem(z + deep - n, deep), y, core)
        arrived(slot)
        push(out.at[slot], slot, send_y.at[n], to_y)
        push(out.at[slot], slot, send_c.at[n], to_c)
    for n in range(deep):
        slot = spot(lax.rem(z + deep - n, deep), 1 - y, core)
        arrived(slot)
        push(out.at[slot], slot, send_c.at[deep + n], to_c)
    for n in range(deep):
        for yy in (y, 1 - y):
            arrived(spot(lax.rem(z + deep - n, deep), yy, 1 - core))
    keep.wait()
    for copy in sends:
        copy.wait_send()


def gather_line(block, number):
    count = lax.axis_size("sp")
    deep = count // 4
    dma = pltpu.SemaphoreType.DMA
    return pl.pallas_call(
        functools.partial(line_kernel, count),
        out_shape=jax.ShapeDtypeStruct((count,) + block.shape, block.dtype),
        in_specs=[VMEM],
        out_specs=VMEM,
        scratch_shapes=[dma, dma((count,)), dma((max(deep - 1, 1),)), dma((deep,)), dma((2 * deep,))],
        compiler_params=pltpu.CompilerParams(
            collective_id=number, has_side_effects=True, vmem_limit_bytes=ROOM
        ),
    )(block)


def swap_kernel(count, split, *refs):
    kinds = len(split)
    ins, outs = refs[:kinds], refs[kinds : 2 * kinds]
    local, send, recv = refs[2 * kinds :]
    here, me = lax.axis_index("sp"), lax.axis_index("flt")
    peers = [lax.rem(me + step, count) for step in range(1, count)]
    greet([(here, peer) for peer in peers])
    sends, keeps = [], []
    for k in range(kinds):
        for n, peer in enumerate(peers):
            src = ins[k].at[peer] if split[k] else ins[k]
            copy = remote(src, outs[k].at[me], send.at[k, n], recv.at[k, me], (here, peer))
            copy.start()
            sends.append(copy)
        keep = pltpu.make_async_copy(ins[k].at[me] if split[k] else ins[k], outs[k].at[me], local.at[k])
        keep.start()
        keeps.append(keep)
    for k in range(kinds):
        for n, peer in enumerate(peers):
            src = ins[k].at[peer] if split[k] else ins[k]
            remote(src, outs[k].at[peer], send.at[k, n], recv.at[k, peer], (here, peer)).wait_recv()
    for copy in sends:
        copy.wait_send()
    for keep in keeps:
        keep.wait()


def swap(number, *pieces):
    count = lax.axis_size("flt")
    split = tuple(cut for _, cut in pieces)
    arrays = [array for array, _ in pieces]
    dma = pltpu.SemaphoreType.DMA
    shapes = [a.shape if cut else (count,) + a.shape for a, cut in pieces]
    return pl.pallas_call(
        functools.partial(swap_kernel, count, split),
        out_shape=[jax.ShapeDtypeStruct(s, a.dtype) for s, a in zip(shapes, arrays)],
        in_specs=[VMEM] * len(arrays),
        out_specs=[VMEM] * len(arrays),
        scratch_shapes=[
            dma((len(arrays),)),
            dma((len(arrays), max(count - 1, 1))),
            dma((len(arrays), count)),
        ],
        compiler_params=pltpu.CompilerParams(
            collective_id=number, has_side_effects=True, vmem_limit_bytes=ROOM
        ),
    )(*arrays)


def first_kernel(high, wide, x_ref, e_ref, out_ref, moved):
    planes, flat, outs = e_ref.shape
    lane = lax.broadcasted_iota(jnp.int32, (outs, flat), 1)
    row, col = lane // wide, lane % wide
    blank = jnp.zeros((9 * outs, flat), jnp.bfloat16)
    moved[:, 0:flat] = blank
    moved[:, (planes + 1) * flat : (planes + 2) * flat] = blank

    def fill(plane, carry):
        errors = jnp.transpose(e_ref[plane].astype(jnp.float32))
        start = pl.multiple_of((plane + 1) * flat, flat)
        for ky in range(3):
            for kz in range(3):
                by = (ky - 1) * wide + (kz - 1)
                there_y, there_z = row - (ky - 1), col - (kz - 1)
                inside = (there_y >= 0) & (there_y < high) & (there_z >= 0) & (there_z < wide)
                turned_by = pltpu.roll(errors, by % flat, 1) if by else errors
                at = (ky * 3 + kz) * outs
                moved[at : at + outs, pl.ds(start, flat)] = jnp.where(inside, turned_by, 0.0).astype(
                    jnp.bfloat16
                )
        return carry

    lax.fori_loop(0, planes, fill, 0)

    def tap(step, carry):
        kx, ky = step // 3, step % 3
        left = moved[
            pl.ds(pl.multiple_of(ky * 3 * outs, 3 * outs), 3 * outs),
            pl.ds(pl.multiple_of((2 - kx) * flat, flat), planes * flat),
        ]
        out_ref[step] = jnp.dot(left, x_ref[...], preferred_element_type=jnp.float32)
        return carry

    lax.fori_loop(0, 9, tap, 0)


def first_grad(x_cells, errors, high, wide):
    planes, flat, outs = errors.shape
    ins = x_cells.shape[1]
    found = pl.pallas_call(
        functools.partial(first_kernel, high, wide),
        out_shape=jax.ShapeDtypeStruct((9, 3 * outs, ins), jnp.float32),
        in_specs=[VMEM, VMEM],
        out_specs=VMEM,
        scratch_shapes=[pltpu.VMEM((9 * outs, (planes + 2) * flat), jnp.bfloat16)],
        compiler_params=pltpu.CompilerParams(vmem_limit_bytes=ROOM),
        cost_estimate=pl.CostEstimate(
            flops=54 * outs * ins * planes * flat, bytes_accessed=8 * planes * flat * ins, transcendentals=0
        ),
    )(x_cells, errors)
    return jnp.transpose(found.reshape(3, 3, 3, outs, ins), (3, 0, 1, 2, 4))


def second_kernel(high, wide, h_ref, e_ref, out_ref):
    rows, _, flat, ins = h_ref.shape
    cells, outs = e_ref.shape
    errors = jnp.transpose(e_ref[...].astype(jnp.float32))
    lane = lax.broadcasted_iota(jnp.int32, (outs, cells), 1)
    col, line, deep = lane % wide, (lane // wide) % high, lane // flat
    found = {}
    for a in range(2):
        for b in range(2):
            for c in range(2):
                by = a * flat + b * wide + c
                ok = (deep + a < rows) & (line + b < high) & (col + c < wide)
                rolled = pltpu.roll(errors, (cells - by) % cells, 1) if by else errors
                found[a, b, c] = jnp.where(ok, rolled, 0.0).astype(jnp.bfloat16)
    for kx in range(3):
        for ky in range(3):
            for kz in range(3):
                kind = ((kx + 1) % 2 * 2 + (ky + 1) % 2) * 2 + (kz + 1) % 2
                left = found[int(kx == 0), int(ky == 0), int(kz == 0)]
                right = h_ref[:, kind].reshape(cells, ins)
                out_ref[(kx * 3 + ky) * 3 + kz] = jnp.dot(
                    left, right, preferred_element_type=jnp.float32
                )


def second_grad(hidden, errors, high, wide):
    rows, _, flat, ins = hidden.shape
    cells, outs = errors.shape
    found = pl.pallas_call(
        functools.partial(second_kernel, high, wide),
        out_shape=jax.ShapeDtypeStruct((27, outs, ins), jnp.float32),
        in_specs=[VMEM, VMEM],
        out_specs=VMEM,
        compiler_params=pltpu.CompilerParams(vmem_limit_bytes=ROOM),
        cost_estimate=pl.CostEstimate(
            flops=54 * outs * ins * cells, bytes_accessed=32 * cells * ins, transcendentals=0
        ),
    )(hidden, errors)
    return jnp.transpose(found.reshape(3, 3, 3, outs, ins), (3, 0, 1, 2, 4))


def shifted(shard, by):
    peers = lax.axis_size("sp")
    pairs = [(i, i + by) for i in range(peers) if 0 <= i + by < peers]
    return lax.ppermute(shard, "sp", pairs)


def conv_plain(field, kernel, strides, pads, dilate):
    return lax.conv_general_dilated(
        field[None],
        kernel,
        strides,
        pads,
        lhs_dilation=dilate,
        dimension_numbers=("NDHWC", "DHWIO", "NDHWC"),
        preferred_element_type=jnp.float32,
    )[0]


def silu_slope(value):
    sig = jax.nn.sigmoid(value)
    return sig * (1.0 + value * (1.0 - sig))


def forward_taps(kernel):
    return jnp.transpose(kernel, (1, 2, 3, 4, 0))


def turned(kernel):
    return jnp.transpose(kernel[:, ::-1, ::-1, ::-1], (1, 2, 3, 0, 4))


def window(whole, below, above, start, size):
    padded = jnp.pad(whole, ((below, above),) + ((0, 0),) * (whole.ndim - 1))
    return lax.dynamic_slice_in_dim(padded, start, size, 0)


def cut_last(array, count):
    parts = array.reshape(array.shape[:-1] + (count, array.shape[-1] // count))
    return jnp.moveaxis(parts, -2, 0)


def cut_rows(array, count):
    parts = array.reshape((array.shape[0], count, array.shape[1] // count) + array.shape[2:])
    return jnp.moveaxis(parts, 1, 0)


def join_rows(parts):
    moved = jnp.moveaxis(parts, 0, 1)
    return moved.reshape((moved.shape[0], moved.shape[1] * moved.shape[2]) + moved.shape[3:])


def join_last(parts):
    moved = jnp.moveaxis(parts, 0, -2)
    return moved.reshape(moved.shape[:-2] + (moved.shape[-2] * moved.shape[-1],))


def own_term(parts_f32, parts_sent, me):
    mine = lax.broadcasted_iota(jnp.int32, (parts_sent.shape[0],) + (1,) * (parts_sent.ndim - 1), 0) == me
    rest = jnp.sum(jnp.where(mine, 0.0, parts_sent.astype(jnp.float32)), 0)
    return rest + lax.dynamic_index_in_dim(parts_f32, me, 0, keepdims=False)


def per_device(activations, w_first, w_second, cotangent):
    planes = activations.shape[0]
    rows = cotangent.shape[0]
    place, me = lax.axis_index("sp"), lax.axis_index("flt")
    count = lax.axis_size("flt")
    line = lax.axis_size("sp")
    single = (1, 1, 1)
    double = (2, 2, 2)
    x_parts, cot_parts = swap(1, (activations, False), (cut_last(cotangent, count), True))
    x_wide, cot_part = join_rows(x_parts), join_rows(cot_parts)
    high, wide = x_wide.shape[1], x_wide.shape[2]
    ins = x_wide.shape[3]
    x_full = lax.all_gather(x_wide, "sp", axis=0, tiled=True)
    x_near = jnp.concatenate([shifted(x_wide, 1), x_wide, shifted(x_wide[:1], -1)], 0)
    first_pre = conv_plain(x_near, forward_taps(w_first), single, ((0, 0), (1, 1), (1, 1)), single)
    plane = lax.broadcasted_iota(jnp.int32, (planes + 1, 1, 1, 1), 0) + place * planes
    hidden = jnp.where(plane > 0, jax.nn.silu(first_pre), 0.0).astype(jnp.bfloat16)
    (h_parts,) = swap(2, (hidden, False))
    h_wide = join_last(h_parts)
    h_own = h_wide[1:].reshape(rows, 2, high // 2, 2, wide // 2, 2, ins)
    h_own = jnp.transpose(h_own, (0, 1, 3, 5, 2, 4, 6)).reshape(rows, 8, high * wide // 4, ins)
    h_full = lax.all_gather(h_own, "sp", axis=0, tiled=True)
    second_pre = conv_plain(
        h_wide, forward_taps(w_second), double, ((0, 0), (1, 0), (1, 0)), single
    )
    second_err = (cot_part.astype(jnp.float32) * silu_slope(second_pre)).astype(jnp.bfloat16)
    outs = second_err.shape[-1]
    e_full = gather_line(second_err.reshape(-1, outs), 3).reshape((line * rows,) + second_err.shape[1:])
    e_near = window(e_full, 0, 1, place * rows, rows + 1)
    back_hidden = conv_plain(e_near, turned(w_second), single, ((1, 0), (1, 2), (1, 2)), double)
    back_parts = cut_last(back_hidden, count)
    section_parts = cut_rows(jax.nn.silu(second_pre), count)
    got, section_got = swap(4, (back_parts.astype(jnp.bfloat16), True), (section_parts, True))
    section_out = join_last(section_got)
    hidden_err = own_term(back_parts, got, me)
    first_err = (hidden_err * silu_slope(first_pre[1:])).astype(jnp.bfloat16)
    f_full = gather_line(first_err.reshape(planes, high * wide, outs), 5)
    f_full = f_full.reshape(line * planes, high * wide, outs)
    f_near = window(f_full, 1, 1, place * planes, planes + 2).reshape(planes + 2, high, wide, outs)
    back_input = conv_plain(f_near, turned(w_first), single, ((0, 0), (1, 1), (1, 1)), single)
    in_parts = cut_rows(back_input, count)
    (in_got,) = swap(6, (in_parts.astype(jnp.bfloat16), True))
    grad_input = own_term(in_parts, in_got, me)
    grad_second = second_grad(h_full, e_full.reshape(-1, outs), high // 2, wide // 2)
    grad_first = first_grad(x_full.reshape(-1, ins), f_full, high, wide)
    return (section_out, grad_input, grad_first, grad_second)


def solution(mesh):
    placed = (
        P("sp", "flt", None, None),
        P("flt", None, None, None, None),
        P("flt", None, None, None, None),
        P("sp", "flt", None, None),
    )
    return jax.shard_map(
        per_device,
        mesh=mesh,
        in_specs=placed,
        out_specs=(
            P("sp", "flt", None, None),
            P("sp", "flt", None, None),
            P("flt", None, None, None, None),
            P("flt", None, None, None, None),
        ),
        check_vma=False,
    )
```
